32 devices in a mesh: region: 8 (over z, x), batch: 4 (over y, core).
Axes of the slice: x: 2, y: 2, z: 4, core: 2. Of those that a mesh axis runs over, the one named last changes fastest.
Arguments:
- features: bfloat16 [8, 63, 32768], P('region', None, 'batch'), may hold values from -1 to 1
- spacing: float32 [8, 32768], P('region', 'batch'), may hold values from 0.000546875 to 0.59375
- counts: int32 [8, 512], P('region', 'batch'), may hold values from 0 to 64, as said below
- depth_rank: int32 [512, 8], P('batch'), may hold values from 0 to 7, each once within a row
- target: float32 [3, 512], P(None, 'batch'), may hold values from 0 to 1
- w_in: float32 [8, 64, 256], P('region', 'batch'), may hold values from -0.75 to 0.75
- w_hid: float32 [8, 2, 256, 256], P('region', None, 'batch'), may hold values from -0.375 to 0.375
- b_hid: float32 [8, 2, 256], P('region', None, 'batch'), may hold values from -1.2 to 1.2
- w_out: float32 [8, 4, 256], P('region', None, 'batch'), may hold values from -0.375 to 0.375
- mom_in: float32 [2, 8, 64, 256], P(None, 'region', 'batch'), may hold values from -1 to 4, as said below
- mom_hid: float32 [2, 8, 2, 256, 256], P(None, 'region', None, 'batch'), may hold values from -1 to 4, as said below
- mom_bias: float32 [2, 8, 2, 256], P(None, 'region', None, 'batch'), may hold values from -1 to 4, as said below
- mom_out: float32 [2, 8, 4, 256], P(None, 'region', None, 'batch'), may hold values from -1 to 4, as said below
Outputs:
- new_w_in: float32 [8, 64, 256], P('region')
- new_w_hid: float32 [8, 2, 256, 256], P('region')
- new_b_hid: float32 [8, 2, 256], P('region')
- new_w_out: float32 [8, 4, 256], P('region')
- new_mom_in: float32 [2, 8, 64, 256], P(None, 'region', 'batch')
- new_mom_hid: float32 [2, 8, 2, 256, 256], P(None, 'region', None, 'batch')
- new_mom_bias: float32 [2, 8, 2, 256], P(None, 'region', None, 'batch')
- new_mom_out: float32 [2, 8, 4, 256], P(None, 'region', None, 'batch')
The draws below stay inside these ranges and needn't reach their ends.
Inputs may be any that keep to these rules, and one draw needn't show every extreme that they name: The first counts[c, ray] slots of a segment are live. `mom_in`: slice 0 is the first moment, slice 1 the second moment, which lies between 0.1 and 4. `mom_hid`: as for mom_in. `mom_bias`: as for mom_in. `mom_out`: as for mom_in.
All inputs are finite; a program needn't handle non-finite values.
Results may differ from the reference program's by a relative error of at most 0.012.
The reference program's roundings to bfloat16 on the way (of `act_one`, `act_two`, `act_three`, `grad_heads`, `back_three`, `back_two` and `back_one`) count: a program that leaves them out, or rounds other values in their place, can miss the bound.
Values may be sent and summed in bfloat16 or wider, within the bound.
A program may use at most 128 MiB of HBM per device.

```python
import jax
import jax.numpy as jnp
from jax import lax

ENC = 63
HID = 256
S = 64
CELLS = 8
RAYS = 512


def draw_counts(key, part):
    key_top, key_choose, key_fill = jax.random.split(jax.random.fold_in(key, 5), 3)
    ceiling = jax.random.randint(key_top, (CELLS,), S // 8, S + 1)
    chosen = jax.random.permutation(key_choose, CELLS)
    ceiling = jnp.where(chosen == 0, S, ceiling)
    filled = jax.random.randint(key_fill, (CELLS, RAYS), 0, ceiling[:, None] + 1)
    filled = filled.at[:, 0].set(ceiling)
    return filled.astype(jnp.int32)


def draw_spacing(key, part):
    key_choose, key_levels, key_rough = jax.random.split(jax.random.fold_in(key, 7), 3)
    chooser = jax.random.uniform(key_choose, (CELLS, RAYS), jnp.float32)
    levels = jax.random.uniform(key_levels, (CELLS, RAYS), jnp.float32)
    rough_draw = jax.random.uniform(key_rough, (CELLS, RAYS, S), jnp.float32)
    lowest_depth = 2.0
    highest_depth = 10.0
    roughness = jnp.exp(jnp.log(0.5) + rough_draw * (jnp.log(2.0) - jnp.log(0.5)))
    dense_depth = jnp.exp(jnp.log(lowest_depth) + levels * (jnp.log(highest_depth) - jnp.log(lowest_depth)))
    thin_depth = jnp.exp(jnp.log(0.5) + levels * (jnp.log(4.0) - jnp.log(0.5))) / CELLS
    seg_depth = jnp.where(chooser < 2.0 / CELLS, dense_depth, thin_depth)
    intervals = seg_depth[:, :, None] * roughness / (0.7 * S)
    return intervals.reshape(CELLS, RAYS * S).astype(jnp.float32)


def moment_pair(key, shape):
    key_first, key_second = jax.random.split(key)
    first = jnp.clip(0.15 * jax.random.normal(key_first, shape, jnp.float32), -1.0, 1.0)
    second = jnp.exp(jax.random.uniform(key_second, shape, jnp.float32, jnp.log(0.25), jnp.log(4.0)))
    return jnp.stack([first, second])


def draw_mom_in(key, part):
    return moment_pair(jax.random.fold_in(key, 11), (CELLS, ENC + 1, HID))


def draw_mom_hid(key, part):
    return moment_pair(jax.random.fold_in(key, 12), (CELLS, 2, HID, HID))


def draw_mom_bias(key, part):
    return moment_pair(jax.random.fold_in(key, 13), (CELLS, 2, HID))


def draw_mom_out(key, part):
    return moment_pair(jax.random.fold_in(key, 14), (CELLS, 4, HID))


def steps_of(stream_key, dims, cuts, least, top_value):
    gain, own = 1.0, jax.random.fold_in(stream_key, 6)
    for axis_at, blocks in cuts:
        draws = jnp.exp(jax.random.uniform(jax.random.fold_in(own, axis_at), (blocks,), jnp.float32, least / len(cuts), top_value / len(cuts)))
        gain = gain * jnp.repeat(draws, dims[axis_at] // blocks).reshape([-1 if axis == axis_at else 1 for axis in range(len(dims))])
    return gain


def normal_values(key, extent, scale, limit, cuts=(), held_as=jnp.bfloat16):
    level = steps_of(key, extent, cuts, -0.22, 0.18) if cuts else 1.0
    entries = jax.random.normal(key, extent, jnp.float32) * scale * level
    return jnp.minimum(jnp.maximum(entries, -limit), limit).astype(held_as)


def setup_inputs(seed: int = 0) -> dict:
    arg_keys = jax.random.split(jax.random.key(seed), 14)
    features = jnp.clip(jax.random.uniform(arg_keys[0], (CELLS, ENC, RAYS * S), jnp.float32, -1.0, 1.0) * steps_of(arg_keys[0], (CELLS, ENC, RAYS * S), ((0, 8), (2, 4)), -0.4, 0.0), -1.0, 1.0).astype(jnp.bfloat16)
    spacing = draw_spacing(jax.random.fold_in(arg_keys[13], 71), 0)
    counts = draw_counts(jax.random.fold_in(arg_keys[13], 71), 0)
    depth_rank = jax.vmap(lambda own: jax.random.permutation(own, CELLS))(jax.random.split(arg_keys[3], RAYS)).reshape((RAYS, CELLS)).astype(jnp.int32)
    target = jnp.clip(1.0 * jax.random.uniform(arg_keys[4], (3, RAYS), jnp.float32) ** steps_of(arg_keys[4], (3, RAYS), ((1, 4),), -0.2, 0.2), 0.0, 1.0)
    w_in = normal_values(arg_keys[5], (CELLS, ENC + 1, HID), (ENC + 1) ** -0.5, 0.75, ((0, 8), (1, 4)), jnp.float32)
    w_hid = normal_values(arg_keys[6], (CELLS, 2, HID, HID), HID ** -0.5, 0.375, ((0, 8), (2, 4)), jnp.float32)
    b_hid = normal_values(arg_keys[7], (CELLS, 2, HID), 0.3, 1.2, ((0, 8), (2, 4)), jnp.float32)
    w_out = normal_values(arg_keys[8], (CELLS, 4, HID), HID ** -0.5, 0.375, ((0, 8), (2, 4)), jnp.float32)
    mom_in = draw_mom_in(jax.random.fold_in(arg_keys[13], 71), 0)
    mom_hid = draw_mom_hid(jax.random.fold_in(arg_keys[13], 71), 0)
    mom_bias = draw_mom_bias(jax.random.fold_in(arg_keys[13], 71), 0)
    mom_out = draw_mom_out(jax.random.fold_in(arg_keys[13], 71), 0)
    return {"features": features, "spacing": spacing, "counts": counts, "depth_rank": depth_rank, "target": target, "w_in": w_in, "w_hid": w_hid, "b_hid": b_hid, "w_out": w_out, "mom_in": mom_in, "mom_hid": mom_hid, "mom_bias": mom_bias, "mom_out": mom_out}


beta_first = 0.9
beta_second = 0.95
learn_rate = 0.01
norm_eps = 1e-06
adam_eps = 1e-08

def contract_first(left, right):
    return lax.dot_general(left, right, (((0,), (0,)), ((), ())), preferred_element_type=jnp.float32)

def contract_last(left, right):
    return lax.dot_general(left, right, (((1,), (1,)), ((), ())), preferred_element_type=jnp.float32)

def network(samples, wide_in, wide_hid, bias_hid, wide_out):
    enc_rows = samples.shape[0]
    pre_one = contract_first(wide_in[:enc_rows], samples) + wide_in[enc_rows][:, None].astype(jnp.float32)
    act_one = jnp.maximum(pre_one, 0.0).astype(jnp.bfloat16)
    pre_two = contract_first(wide_hid[0], act_one) + bias_hid[0][:, None]
    act_two = jnp.maximum(pre_two, 0.0).astype(jnp.bfloat16)
    pre_three = contract_first(wide_hid[1], act_two) + bias_hid[1][:, None]
    act_three = jnp.maximum(pre_three, 0.0).astype(jnp.bfloat16)
    heads = jnp.dot(wide_out, act_three, preferred_element_type=jnp.float32)
    return ((pre_one, act_one, pre_two, act_two, pre_three, act_three), heads)

def optical(heads, gaps, live_counts):
    rays = live_counts.shape[0]
    slot = lax.broadcasted_iota(jnp.int32, (rays, S), 1)
    live = (slot < live_counts[:, None]).astype(jnp.float32)
    density = jax.nn.softplus(heads[0]).reshape(rays, S)
    depth = density * gaps.reshape(rays, S) * live
    colours = jax.nn.sigmoid(heads[1:4])
    return (live, depth, colours)

def summarize(depth, colours):
    rays = depth.shape[0]
    cum_in = jnp.cumsum(depth, axis=1)
    weight = jnp.exp(-(cum_in - depth)) * -jnp.expm1(-depth)
    shade = colours.reshape(3, rays, S)
    seg_colour = lax.optimization_barrier(jnp.sum(weight[None] * shade, axis=2))
    log_trans = -cum_in[:, -1]
    return (seg_colour, log_trans, cum_in, weight)

def backward(samples, gaps, live, depth, cum_in, weight, colours, heads, acts, mats, grad_seg, grad_log):
    pre_one, act_one, pre_two, act_two, pre_three, act_three = acts
    wide_in, wide_hid, wide_out = mats
    rays = depth.shape[0]
    shade = colours.reshape(3, rays, S)
    emit = lax.optimization_barrier(jnp.sum(grad_seg[:, :, None] * shade, axis=0))
    carried = emit * weight
    after = lax.optimization_barrier(jnp.sum(carried, axis=1, keepdims=True)) - jnp.cumsum(carried, axis=1)
    grad_depth = emit * jnp.exp(-cum_in) - after - grad_log[:, None]
    grad_density = (grad_depth * live * gaps.reshape(rays, S)).reshape(1, -1) * jax.nn.sigmoid(heads[0:1])
    grad_shade = (grad_seg[:, :, None] * weight[None]).reshape(3, -1) * colours * (1.0 - colours)
    grad_heads = jnp.concatenate([grad_density, grad_shade], axis=0).astype(jnp.bfloat16)
    grad_out = contract_last(grad_heads, act_three)
    back_three = jnp.where(pre_three > 0, contract_first(wide_out, grad_heads), 0.0).astype(jnp.bfloat16)
    grad_third = contract_last(act_two, back_three)
    bias_third = lax.optimization_barrier(jnp.sum(back_three.astype(jnp.float32), axis=1))
    back_two = jnp.where(pre_two > 0, jnp.dot(wide_hid[1], back_three, preferred_element_type=jnp.float32), 0.0).astype(jnp.bfloat16)
    grad_second = contract_last(act_one, back_two)
    bias_second = lax.optimization_barrier(jnp.sum(back_two.astype(jnp.float32), axis=1))
    back_one = jnp.where(pre_one > 0, jnp.dot(wide_hid[0], back_two, preferred_element_type=jnp.float32), 0.0).astype(jnp.bfloat16)
    grad_first = contract_last(samples, back_one)
    bias_first = lax.optimization_barrier(jnp.sum(back_one.astype(jnp.float32), axis=1))
    grad_in = jnp.concatenate([grad_first, bias_first[None]], axis=0)
    grad_hid = jnp.stack([grad_second, grad_third])
    grad_bias = jnp.stack([bias_second, bias_third])
    return (grad_in, grad_hid, grad_bias, grad_out)

def adam_step(grad, param, moment, scale):
    scaled = grad * scale
    first = beta_first * moment[0] + (1.0 - beta_first) * scaled
    second = beta_second * moment[1] + (1.0 - beta_second) * scaled * scaled
    fresh = param - learn_rate * first / (jnp.sqrt(second) + adam_eps)
    return (fresh, jnp.stack([first, second]))

def reference(features, spacing, counts, depth_rank, target, w_in, w_hid, b_hid, w_out, mom_in, mom_hid, mom_bias, mom_out):
    param_count = (ENC + 1) * HID + 2 * HID * HID + 6 * HID

    def forward_cell(items):
        samples, gaps, live_counts, first_w, hid_w, hid_b, last_w = items
        acts, heads = network(samples, first_w.astype(jnp.bfloat16), hid_w.astype(jnp.bfloat16), hid_b, last_w.astype(jnp.bfloat16))
        live, depth, colours = optical(heads, gaps, live_counts)
        seg_colour, log_trans, cum_in, weight = summarize(depth, colours)
        return (seg_colour, log_trans)
    seg_colour, log_trans = lax.map(forward_cell, (features, spacing, counts, w_in, w_hid, b_hid, w_out))
    ranks = depth_rank.T
    earlier = ranks[None, :, :] < ranks[:, None, :]
    prefix = lax.optimization_barrier(jnp.sum(jnp.where(earlier, log_trans[None], 0.0), axis=1))
    reach = jnp.exp(prefix)
    lit = reach[:, None] * seg_colour
    colour = lax.optimization_barrier(jnp.sum(lit, axis=0))
    grad_colour = 2.0 * (colour - target)
    later = ranks[None, :, :] > ranks[:, None, :]
    behind = lax.optimization_barrier(jnp.sum(jnp.where(later[:, :, None, :], lit[None], 0.0), axis=1))
    grad_seg_all = reach[:, None] * grad_colour[None]
    grad_log_all = lax.optimization_barrier(jnp.sum(grad_colour[None] * behind, axis=1))

    def update_cell(items):
        samples, gaps, live_counts, first_w, hid_w, hid_b, last_w, grad_seg, grad_log, m_first, m_hid, m_bias, m_last = items
        mats = (first_w.astype(jnp.bfloat16), hid_w.astype(jnp.bfloat16), last_w.astype(jnp.bfloat16))
        acts, heads = network(samples, mats[0], mats[1], hid_b, mats[2])
        live, depth, colours = optical(heads, gaps, live_counts)
        seg_c, log_t, cum_in, weight = summarize(depth, colours)
        grads = backward(samples, gaps, live, depth, cum_in, weight, colours, heads, acts, mats, grad_seg, grad_log)
        total_sq = jnp.sum(grads[0] * grads[0]) + jnp.sum(grads[1] * grads[1]) + jnp.sum(grads[2] * grads[2]) + jnp.sum(grads[3] * grads[3])
        scale = lax.rsqrt(total_sq / param_count + norm_eps)
        new_in, mom_first = adam_step(grads[0], first_w, m_first, scale)
        new_hid, mom_second = adam_step(grads[1], hid_w, m_hid, scale)
        new_bias, mom_third = adam_step(grads[2], hid_b, m_bias, scale)
        new_out, mom_fourth = adam_step(grads[3], last_w, m_last, scale)
        return (new_in, new_hid, new_bias, new_out, mom_first, mom_second, mom_third, mom_fourth)
    results = lax.map(update_cell, (features, spacing, counts, w_in, w_hid, b_hid, w_out, grad_seg_all, grad_log_all, jnp.moveaxis(mom_in, 0, 1), jnp.moveaxis(mom_hid, 0, 1), jnp.moveaxis(mom_bias, 0, 1), jnp.moveaxis(mom_out, 0, 1)))
    return (results[0], results[1], results[2], results[3], jnp.moveaxis(results[4], 1, 0), jnp.moveaxis(results[5], 1, 0), jnp.moveaxis(results[6], 1, 0), jnp.moveaxis(results[7], 1, 0))
```

```python
import functools

import jax
import jax.numpy as jnp
from jax import lax
from jax.experimental import pallas as pl
from jax.experimental.pallas import tpu as pltpu
from jax.sharding import PartitionSpec as P

MESH = pl.DeviceIdType.MESH
F32 = jnp.float32
BF16 = jnp.bfloat16
LANES = 128
ONES = 16

beta_first = 0.9
beta_second = 0.95
learn_rate = 0.01
norm_eps = 1e-06
adam_eps = 1e-08


def exact_dot(left, right):
    return jnp.dot(left, right, precision=lax.Precision.HIGHEST, preferred_element_type=F32)


def dot_nt(left, right, precision=None):
    return lax.dot_general(
        left, right, (((1,), (1,)), ((), ())), precision=precision, preferred_element_type=F32
    )


def iota(shape, axis):
    return lax.broadcasted_iota(jnp.int32, shape, axis)


def flip(index, bit):
    return index + bit - 2 * bit * ((index // bit) % 2)


def place_of(row, rows_hid, hid):
    return (iota((rows_hid, hid), 1) == iota((rows_hid, hid), 0) + row * rows_hid).astype(F32)


def kernel(
    cfg,
    feat_hbm, gaps_hbm, counts_hbm, ranks_hbm, target_hbm,
    w_in_hbm, w_hid_hbm, b_hid_hbm, w_out_hbm,
    m_in_hbm, m_hid_hbm, m_bias_hbm, m_out_hbm,
    t1, t2, t3, big,
    feat_raw, gaps_ref, counts_ref, ranks_ref, target_ref,
    w_in_ref, w_hid_ref, b_hid_ref, w_out_ref,
    m_in_ref, m_hid_ref, m_bias_ref, m_out_ref,
    feat, act1, act2, act3, back2, heads, gheads, table,
    w1b, w2b, w3b, w1t, w2t, w3t, wot, early,
    g1, g2, g3, acco, r1, r2, s1, s2, y1, y2, z1, z2, d3,
    in_sem, wsend, wrecv, bsend, brecv, tsend, trecv, gsend, grecv, dsend, drecv,
):
    nbatch, nregion, slots, halves, chunk = cfg
    cell = lax.axis_index("region")
    row = lax.axis_index("batch")
    enc, samples = feat_raw.shape
    hid = w2b.shape[0]
    rows_in, rows_hid = w_in_ref.shape[0], w_hid_ref.shape[1]
    block = rows_in + 2 * rows_hid + 8
    part = samples // halves
    grid = part // LANES
    per_row = LANES // slots
    full_in = feat.shape[0]

    barrier = pltpu.get_barrier_semaphore()
    for k in range(1, nbatch):
        pl.semaphore_signal(
            barrier, inc=1, device_id={"batch": lax.rem(row + k, nbatch)}, device_id_type=MESH
        )
    for k in range(1, nregion):
        pl.semaphore_signal(
            barrier, inc=1, device_id={"region": lax.rem(cell + k, nregion)}, device_id_type=MESH
        )

    origins = (
        w_in_hbm, w_out_hbm, b_hid_hbm, w_hid_hbm, feat_hbm, m_out_hbm, m_bias_hbm, m_in_hbm,
        m_hid_hbm, gaps_hbm, counts_hbm, ranks_hbm, target_hbm,
    )
    landings = (
        w_in_ref, w_out_ref, b_hid_ref, w_hid_ref, feat_raw, m_out_ref, m_bias_ref, m_in_ref,
        m_hid_ref, gaps_ref, counts_ref, ranks_ref, target_ref,
    )
    arrivals = [
        pltpu.make_async_copy(src, dst, in_sem.at[i])
        for i, (src, dst) in enumerate(zip(origins, landings))
    ]
    for arrival in arrivals:
        arrival.start()
    act1[hid:hid + ONES, :] = jnp.ones((ONES, samples), BF16)
    act2[hid:hid + ONES, :] = jnp.ones((ONES, samples), BF16)
    gheads[...] = jnp.zeros_like(gheads)
    g1[...] = jnp.zeros_like(g1)
    g2[...] = jnp.zeros_like(g2)
    g3[...] = jnp.zeros_like(g3)
    acco[...] = jnp.zeros_like(acco)
    for arrival in arrivals:
        arrival.wait()

    w1b[pl.ds(row * rows_in, rows_in), :] = w_in_ref[...].astype(BF16)
    w2b[pl.ds(row * rows_hid, rows_hid), :] = w_hid_ref[0].astype(BF16)
    w3b[pl.ds(row * rows_hid, rows_hid), :] = w_hid_ref[1].astype(BF16)
    place = place_of(row, rows_hid, hid)

    def spread(narrow_out, narrow_bias):
        narrow = jnp.concatenate(
            [narrow_out, narrow_bias, jnp.zeros((2, rows_hid), F32)], axis=0
        )
        return exact_dot(narrow, place)

    own_small = spread(w_out_ref[...], b_hid_ref[...])
    early[row] = own_small
    big[row, 0, 0:rows_in] = w_in_ref[...]
    big[row, 0, rows_in:rows_in + rows_hid] = w_hid_ref[0]
    big[row, 0, rows_in + rows_hid:rows_in + 2 * rows_hid] = w_hid_ref[1]
    big[row, 0, rows_in + 2 * rows_hid:block] = own_small
    for kind in range(2):
        big[row, kind + 1, 0:rows_in] = m_in_ref[kind]
        big[row, kind + 1, rows_in:rows_in + rows_hid] = m_hid_ref[kind, 0]
        big[row, kind + 1, rows_in + rows_hid:rows_in + 2 * rows_hid] = m_hid_ref[kind, 1]
        big[row, kind + 1, rows_in + 2 * rows_hid:block] = spread(m_out_ref[kind], m_bias_ref[kind])

    @pl.loop(0, samples // chunk)
    def _(step):
        span = pl.ds(pl.multiple_of(step * chunk, chunk), chunk)
        wide = feat_raw[:, span].astype(F32)
        feat[:, span] = jnp.concatenate([wide, jnp.ones((1, chunk), F32)], axis=0).astype(BF16)

    pl.semaphore_wait(barrier, nbatch - 1 + nregion - 1)

    pieces = (
        lambda d: w1b.at[pl.ds(d * rows_in, rows_in), :],
        lambda d: early.at[d],
        lambda d: w2b.at[pl.ds(d * rows_hid, rows_hid), :],
        lambda d: w3b.at[pl.ds(d * rows_hid, rows_hid), :],
    )

    def weight_copy(piece, k, origin, target):
        ref = pieces[piece](origin)
        return pltpu.make_async_remote_copy(
            src_ref=ref, dst_ref=ref, send_sem=wsend.at[piece, k], recv_sem=wrecv.at[piece, k],
            device_id={"batch": target}, device_id_type=MESH,
        )

    for piece in (0, 2, 1, 3):
        for k in range(1, nbatch):
            weight_copy(piece, k, row, lax.rem(row + k, nbatch)).start()

    def await_weights(piece):
        for k in range(1, nbatch):
            weight_copy(piece, k, lax.rem(row + nbatch - k, nbatch), row).wait_recv()

    bits = []
    while (1 << len(bits)) < nbatch:
        bits.append(1 << len(bits))
    high = bits[::-1]
    blocks = {}
    count = 0
    known = [0]
    for bit in high:
        blocks[bit] = []
        for held in known:
            blocks[bit].append((held, count))
            count += 1
        known = known + [held ^ bit for held in known]

    def offset(index, mask):
        for bit in bits:
            if mask & bit:
                index = flip(index, bit)
        return index

    def block_copy(bit, held, sem, incoming):
        ref = big.at[offset(row, held ^ bit if incoming else held)]
        return pltpu.make_async_remote_copy(
            src_ref=ref, dst_ref=ref, send_sem=bsend.at[sem], recv_sem=brecv.at[sem],
            device_id={"batch": flip(row, bit)}, device_id_type=MESH,
        )

    for bit in high:
        for held, sem in blocks[bit]:
            if held == 0:
                block_copy(bit, held, sem, False).start()

    square = (LANES, LANES)
    first_lane, second_lane = iota(square, 0), iota(square, 1)
    same = first_lane // slots == second_lane // slots
    upto = (same & (first_lane <= second_lane)).astype(F32)
    beyond = (same & (first_lane > second_lane)).astype(F32)
    to_ray = (first_lane // slots == second_lane % per_row).astype(F32)
    to_slot = (first_lane % per_row == second_lane // slots).astype(F32)
    ranks = ranks_ref[...].astype(F32)
    await_weights(0)
    w1t[...] = w1b[...].astype(F32).T.astype(BF16)

    def over(half, body):
        @pl.loop(0, part // chunk)
        def _(step):
            body(pl.ds(pl.multiple_of(half * part + step * chunk, chunk), chunk), step)

    def first(span, step):
        pre = jnp.dot(w1t[...], feat[:, span], preferred_element_type=F32)
        act1[0:hid, span] = jnp.maximum(pre, 0.0).astype(BF16)

    for half in range(halves):
        over(half, first)
    await_weights(1)
    small = early[0]
    for d in range(1, nbatch):
        small = small + early[d]
    wide_out = small.astype(BF16)
    tall = small.T
    wot[...] = tall.astype(BF16)
    bias_two, bias_three = tall[:, 4:5], tall[:, 5:6]

    def forward(half):
        def second(span, step):
            pre = jnp.dot(w2t[...], act1[0:hid, span], preferred_element_type=F32) + bias_two
            act2[0:hid, span] = jnp.maximum(pre, 0.0).astype(BF16)

        def third(span, step):
            pre = jnp.dot(w3t[...], act2[0:hid, span], preferred_element_type=F32) + bias_three
            act = jnp.maximum(pre, 0.0).astype(BF16)
            act3[:, span] = act
            out = jnp.dot(wide_out, act, preferred_element_type=F32)
            for t in range(chunk // LANES):
                at = half * grid * 8 + step * (chunk // LANES * 8) + t * 8
                heads[pl.ds(pl.multiple_of(at, 8), 8), :] = out[:, t * LANES:(t + 1) * LANES]

        if half == 0:
            await_weights(2)
            w2t[...] = w2b[...].astype(F32).T.astype(BF16)
        over(half, second)
        if half == 0:
            await_weights(3)
            w3t[...] = w3b[...].astype(F32).T.astype(BF16)
        over(half, third)

    def optical(half):
        raw = [heads[pl.ds(half * grid * 8 + k, grid, stride=8), :] for k in range(4)]
        gaps = gaps_ref[half * grid:(half + 1) * grid, :]
        lane, line = iota((grid, LANES), 1), iota((grid, LANES), 0)
        mine = lane // per_row == line + half * grid
        counted = exact_dot(jnp.where(mine, counts_ref[...].astype(F32), 0.0), to_slot)
        live = ((lane % slots).astype(F32) < counted - 0.5).astype(F32)
        softplus = jnp.maximum(raw[0], 0.0) + jnp.log1p(jnp.exp(-jnp.abs(raw[0])))
        depth = softplus * gaps * live
        shade = [jax.nn.sigmoid(raw[k]) for k in (1, 2, 3)]
        cum_in = exact_dot(depth, upto)
        series = depth * (1.0 - depth * (0.5 - depth * (1.0 / 6.0 - depth * (1.0 / 24.0))))
        opacity = jnp.where(depth < 0.02, series, 1.0 - jnp.exp(-depth))
        weight = jnp.exp(-(cum_in - depth)) * opacity
        stacked = jnp.concatenate([weight * shade[k] for k in range(3)] + [-depth], axis=0)
        gathered = exact_dot(stacked, to_ray)
        lines = [
            jnp.sum(
                jnp.where(mine, gathered[k * grid:(k + 1) * grid], 0.0), axis=0, keepdims=True
            )
            for k in range(4)
        ]
        table[half, cell] = jnp.concatenate(lines + [jnp.zeros((4, LANES), F32)], axis=0)
        return mine, gaps, live, raw[0], shade, cum_in, weight

    def table_copy(half, k, origin, target):
        ref = table.at[half, origin]
        return pltpu.make_async_remote_copy(
            src_ref=ref, dst_ref=ref, send_sem=tsend.at[half, k], recv_sem=trecv.at[half, k],
            device_id={"region": target}, device_id_type=MESH,
        )

    def composite(half, kept):
        mine, gaps, live, raw, shade, cum_in, weight = kept
        every = [table[half, :, k, :] for k in range(4)]
        prefix = jnp.zeros((nregion, LANES), F32)
        for j in range(nregion):
            prefix = prefix + jnp.where(ranks[j:j + 1] < ranks, every[3][j:j + 1], 0.0)
        reach = jnp.exp(prefix)
        here = iota((nregion, LANES), 0) == cell
        own_rank = jnp.sum(jnp.where(here, ranks, 0.0), axis=0, keepdims=True)
        own_reach = jnp.sum(jnp.where(here, reach, 0.0), axis=0, keepdims=True)
        later = ranks > own_rank
        grad_log = jnp.zeros((1, LANES), F32)
        per_ray = []
        for k in range(3):
            lit = reach * every[k]
            grad_colour = 2.0 * (jnp.sum(lit, axis=0, keepdims=True) - target_ref[k:k + 1])
            behind = jnp.sum(jnp.where(later, lit, 0.0), axis=0, keepdims=True)
            grad_log = grad_log + grad_colour * behind
            per_ray.append(own_reach * grad_colour)
        stacked = jnp.concatenate(
            [jnp.where(mine, x, 0.0) for x in per_ray + [grad_log]], axis=0
        )
        laid = exact_dot(stacked, to_slot)
        grad_seg = [laid[k * grid:(k + 1) * grid] for k in range(3)]
        emit = grad_seg[0] * shade[0] + grad_seg[1] * shade[1] + grad_seg[2] * shade[2]
        after = exact_dot(emit * weight, beyond)
        grad_depth = emit * jnp.exp(-cum_in) - after - laid[3 * grid:4 * grid]
        base = half * grid * 8
        gheads[pl.ds(base, grid, stride=8), :] = grad_depth * live * gaps * jax.nn.sigmoid(raw)
        for k in range(3):
            gheads[pl.ds(base + k + 1, grid, stride=8), :] = (
                grad_seg[k] * weight * shade[k] * (1.0 - shade[k])
            )

    def backward_three(half):
        def body(span, step):
            tiles = []
            for t in range(chunk // LANES):
                at = half * grid * 8 + step * (chunk // LANES * 8) + t * 8
                tiles.append(gheads[pl.ds(pl.multiple_of(at, 8), 8), :])
            grad_heads = jnp.concatenate(tiles, axis=1).astype(BF16)
            act = act3[:, span]
            acco[...] += dot_nt(grad_heads, act)
            raw = jnp.dot(wot[...], grad_heads, preferred_element_type=F32).astype(BF16)
            back3 = jnp.where(act > 0, raw, jnp.zeros_like(raw))
            g1[...] += dot_nt(act2[:, span], back3)
            raw = jnp.dot(w3b[...], back3, preferred_element_type=F32).astype(BF16)
            back2[:, span] = jnp.where(act2[0:hid, span] > 0, raw, jnp.zeros_like(raw))

        over(half, body)

    def grad_two(half):
        def body(span, step):
            g2[...] += dot_nt(act1[:, span], back2[:, span])

        over(half, body)

    def backward_one(half):
        def body(span, step):
            raw = jnp.dot(w2b[...], back2[:, span], preferred_element_type=F32).astype(BF16)
            back1 = jnp.where(act1[0:hid, span] > 0, raw, jnp.zeros_like(raw))
            g3[...] += dot_nt(feat[:, span], back1)

        over(half, body)

    kept = []
    for half in range(halves):
        forward(half)
        kept.append(optical(half))
        for k in range(1, nregion):
            table_copy(half, k, cell, lax.rem(cell + k, nregion)).start()
    for half in range(halves):
        for k in range(1, nregion):
            table_copy(half, k, lax.rem(cell + nregion - k, nregion), cell).wait_recv()
        composite(half, kept[half])
        backward_three(half)

    side = row % 2
    partner = flip(row, 1)

    def grad_copy(src, dst, sem, target):
        return pltpu.make_async_remote_copy(
            src_ref=src, dst_ref=dst, send_sem=gsend.at[sem], recv_sem=grecv.at[sem],
            device_id={"batch": target}, device_id_type=MESH,
        )

    steps = 2 + len(bits) - 1

    def reduce_start(group, g, r):
        length = r.shape[0]
        away = g.at[pl.ds(pl.multiple_of((1 - side) * length, 8), length), :]
        copy = grad_copy(away, r, group * steps, partner)
        copy.start()
        return copy

    def reduce_across(group, g, r, s, y, copy):
        length = r.shape[0]
        copy.wait_recv()
        near = g[pl.ds(pl.multiple_of(side * length, 8), length), :]
        s[0] = (near + r[...]).astype(BF16)
        return [
            grad_copy(s.at[i], y.at[i], group * steps + 1 + i, flip(row, bit))
            for i, bit in enumerate(bits[1:])
        ]

    def reduce_stages(group, s, y, t, z, copies):
        length = s.shape[1]
        for i, copy in enumerate(copies):
            if i > 0:
                s[i] = total.astype(BF16)
                copy.start()
            copy.wait_recv()
            total = s[i].astype(F32) + y[i].astype(F32)
        span = pl.ds(pl.multiple_of(side * length, 8), length)
        z[side] = total.astype(BF16)
        t[span, :] = total.astype(BF16).astype(F32)
        last = grad_copy(z.at[side], z.at[side], group * steps + steps - 1, partner)
        last.start()
        return last

    def reduce_end(group, t, z):
        length = t.shape[0] // 2
        span = pl.ds(pl.multiple_of((1 - side) * length, 8), length)
        there = z.at[1 - side]
        grad_copy(there, there, group * steps + steps - 1, partner).wait_recv()
        t[span, :] = z[1 - side].astype(F32)

    middle = halves // 2
    g1[hid + 8:hid + ONES, :] = acco[...]
    first_one = reduce_start(0, g1, r1)
    for half in range(middle):
        grad_two(half)
    cross_one = reduce_across(0, g1, r1, s1, y1, first_one)
    for copy in cross_one[:1]:
        copy.start()
    for half in range(middle, halves):
        grad_two(half)
    first_two = reduce_start(1, g2, r2)
    for bit in high[:-1]:
        for held, sem in blocks[bit]:
            block_copy(bit, held, sem, True).wait_recv()
    for held, sem in blocks[high[-1]]:
        if held != 0:
            block_copy(high[-1], held, sem, False).start()
    backward_one(0)
    cross_two = reduce_across(1, g2, r2, s2, y2, first_two)
    for copy in cross_two[:1]:
        copy.start()
    for half in range(1, halves):
        backward_one(half)

    d3[row] = g3[...].astype(BF16)

    def direct_copy(k, origin, target):
        return pltpu.make_async_remote_copy(
            src_ref=d3.at[origin], dst_ref=d3.at[origin], send_sem=dsend.at[k],
            recv_sem=drecv.at[k], device_id={"batch": target}, device_id_type=MESH,
        )

    for k in range(1, nbatch):
        direct_copy(k, row, lax.rem(row + k, nbatch)).start()
    last_one = reduce_stages(0, s1, y1, t1, z1, cross_one)
    last_two = reduce_stages(1, s2, y2, t2, z2, cross_two)
    for k in range(1, nbatch):
        direct_copy(k, lax.rem(row + nbatch - k, nbatch), row).wait_recv()
    total = d3[0].astype(F32)
    for d in range(1, nbatch):
        total = total + d3[d].astype(F32)
    t3[...] = total
    reduce_end(0, t1, z1)
    for held, sem in blocks[high[-1]]:
        block_copy(high[-1], held, sem, True).wait_recv()
    reduce_end(1, t2, z2)

    for piece in range(4):
        for k in range(1, nbatch):
            weight_copy(piece, k, row, lax.rem(row + k, nbatch)).wait_send()
    for bit in high:
        for held, sem in blocks[bit]:
            block_copy(bit, held, sem, False).wait_send()
    for half in range(halves):
        for k in range(1, nregion):
            table_copy(half, k, cell, lax.rem(cell + k, nregion)).wait_send()
    for k in range(1, nbatch):
        direct_copy(k, row, lax.rem(row + k, nbatch)).wait_send()
    for copy in [first_one, first_two, last_one, last_two] + cross_one + cross_two:
        copy.wait_send()


def step_kernel(
    cfg, t1, t2, t3, big, nw_in, nw_hid, nb_hid, nw_out, nm_in, nm_hid, nm_bias, nm_out
):
    nbatch, rows_in, rows_hid = cfg
    row = lax.axis_index("batch")
    full_in, hid = nw_in.shape
    block = big.shape[2]
    place = place_of(row, rows_hid, hid)
    count_all = full_in * hid + 2 * hid * hid + 6 * hid
    last_rows = jnp.concatenate(
        [t1[hid + 8:hid + 12, :], t2[hid:hid + 1, :], t1[hid:hid + 1, :], jnp.zeros((2, hid), F32)],
        axis=0,
    )

    def squares(x):
        return jnp.sum(x * x, axis=0, keepdims=True)

    columns = (
        squares(t1[0:hid, :]) + squares(t2[0:hid, :]) + squares(t3[...])
        + squares(last_rows)
    )
    total_sq = jnp.sum(columns, axis=1, keepdims=True)
    scale = lax.rsqrt(total_sq / count_all + norm_eps)

    def adam(grad, param, first, second):
        scaled = grad * scale
        first = beta_first * first + (1.0 - beta_first) * scaled
        second = beta_second * second + (1.0 - beta_second) * scaled * scaled
        return param - learn_rate * first / (jnp.sqrt(second) + adam_eps), first, second

    def span_of(d, rows, start=0):
        return pl.ds(pl.multiple_of(start + d * rows, 8), rows)

    def update(d, grad, lo, rows):
        return adam(
            grad, big[d, 0, lo:lo + rows], big[d, 1, lo:lo + rows], big[d, 2, lo:lo + rows]
        )

    lo_two, lo_three, lo_small = rows_in, rows_in + rows_hid, rows_in + 2 * rows_hid
    for d in range(nbatch):
        at_in = slice(d * rows_in, (d + 1) * rows_in)
        at_hid = slice(d * rows_hid, (d + 1) * rows_hid)
        nw_in[at_in, :] = update(d, t3[at_in, :], 0, rows_in)[0]
        nw_hid[0, at_hid, :] = update(d, t2[at_hid, :], lo_two, rows_hid)[0]
        nw_hid[1, at_hid, :] = update(d, t1[at_hid, :], lo_three, rows_hid)[0]
    whole = []
    for kind in range(3):
        value = big[0, kind, lo_small:block]
        for d in range(1, nbatch):
            value = value + big[d, kind, lo_small:block]
        whole.append(value)
    fresh, first, second = adam(last_rows, *whole)
    nw_out[...] = fresh[0:4]
    nb_hid[...] = fresh[4:6]
    for kind, value in enumerate((first, second)):
        narrow = dot_nt(value, place, lax.Precision.HIGHEST)
        nm_out[kind] = narrow[0:4]
        nm_bias[kind] = narrow[4:6]
    _, first, second = update(row, t3[span_of(row, rows_in), :], 0, rows_in)
    nm_in[0], nm_in[1] = first, second
    _, first, second = update(row, t2[span_of(row, rows_hid), :], lo_two, rows_hid)
    nm_hid[0, 0], nm_hid[1, 0] = first, second
    _, first, second = update(row, t1[span_of(row, rows_hid), :], lo_three, rows_hid)
    nm_hid[0, 1], nm_hid[1, 1] = first, second


def body(
    features, spacing, counts, depth_rank, target, w_in, w_hid, b_hid, w_out,
    mom_in, mom_hid, mom_bias, mom_out,
):
    nbatch, nregion = lax.axis_size("batch"), lax.axis_size("region")
    _, enc, samples = features.shape
    rays = counts.shape[1]
    slots = samples // rays
    hid = w_in.shape[2]
    rows_in, rows_hid = w_in.shape[1], w_hid.shape[2]
    full_in = rows_in * nbatch
    halves = 2
    chunk = min(2048, samples // halves)
    block = rows_in + 2 * rows_hid + 8
    levels = nbatch.bit_length() - 1
    len1 = (hid + ONES) // 2
    len2 = len1
    cfg = (nbatch, nregion, slots, halves, chunk)
    vmem = pl.BlockSpec(memory_space=pltpu.VMEM)
    shape = lambda *dims: jax.ShapeDtypeStruct(dims, F32)
    dma = pltpu.SemaphoreType.DMA
    crossing = max(levels - 1, 1)
    sums = pl.pallas_call(
        functools.partial(kernel, cfg),
        out_shape=(
            pltpu.VMEM((2 * len1, hid), F32), pltpu.VMEM((2 * len2, hid), F32),
            pltpu.VMEM((full_in, hid), F32), pltpu.VMEM((nbatch, 3, block, hid), F32),
        ),
        in_specs=[pl.BlockSpec(memory_space=pltpu.HBM)] * 13,
        out_specs=(vmem,) * 4,
        scratch_shapes=[
            pltpu.VMEM((enc, samples), BF16),
            pltpu.VMEM((samples // LANES, LANES), F32),
            pltpu.VMEM(counts.shape, jnp.int32),
            pltpu.VMEM((nregion, rays), jnp.int32),
            pltpu.VMEM(target.shape, F32),
            pltpu.VMEM(w_in.shape[1:], F32),
            pltpu.VMEM(w_hid.shape[1:], F32),
            pltpu.VMEM(b_hid.shape[1:], F32),
            pltpu.VMEM(w_out.shape[1:], F32),
            pltpu.VMEM((2,) + mom_in.shape[2:], F32),
            pltpu.VMEM((2,) + mom_hid.shape[2:], F32),
            pltpu.VMEM((2,) + mom_bias.shape[2:], F32),
            pltpu.VMEM((2,) + mom_out.shape[2:], F32),
            pltpu.VMEM((full_in, samples), BF16),
            pltpu.VMEM((hid + ONES, samples), BF16),
            pltpu.VMEM((hid + ONES, samples), BF16),
            pltpu.VMEM((hid, samples), BF16),
            pltpu.VMEM((hid, samples), BF16),
            pltpu.VMEM((samples // LANES * 8, LANES), F32),
            pltpu.VMEM((samples // LANES * 8, LANES), F32),
            pltpu.VMEM((halves, nregion, 8, LANES), F32),
            pltpu.VMEM((full_in, hid), BF16),
            pltpu.VMEM((hid, hid), BF16),
            pltpu.VMEM((hid, hid), BF16),
            pltpu.VMEM((hid, full_in), BF16),
            pltpu.VMEM((hid, hid), BF16),
            pltpu.VMEM((hid, hid), BF16),
            pltpu.VMEM((hid, 8), BF16),
            pltpu.VMEM((nbatch, 8, hid), F32),
            pltpu.VMEM((2 * len1, hid), F32),
            pltpu.VMEM((2 * len2, hid), F32),
            pltpu.VMEM((full_in, hid), F32),
            pltpu.VMEM((8, hid), F32),
            pltpu.VMEM((len1, hid), F32),
            pltpu.VMEM((len2, hid), F32),
            pltpu.VMEM((crossing, len1, hid), BF16),
            pltpu.VMEM((crossing, len2, hid), BF16),
            pltpu.VMEM((crossing, len1, hid), BF16),
            pltpu.VMEM((crossing, len2, hid), BF16),
            pltpu.VMEM((2, len1, hid), BF16),
            pltpu.VMEM((2, len2, hid), BF16),
            pltpu.VMEM((nbatch, full_in, hid), BF16),
            dma((13,)),
            dma((4, nbatch)),
            dma((4, nbatch)),
            dma((nbatch,)),
            dma((nbatch,)),
            dma((halves, nregion)),
            dma((halves, nregion)),
            dma((2 * (levels + 1),)),
            dma((2 * (levels + 1),)),
            dma((nbatch,)),
            dma((nbatch,)),
        ],
        compiler_params=pltpu.CompilerParams(
            collective_id=0, has_side_effects=True, vmem_limit_bytes=44 * 1024 * 1024
        ),
        name="window",
    )(*[
        pltpu.with_memory_space_constraint(x, pltpu.HBM) for x in (
            features[0], spacing.reshape(samples // LANES, LANES), counts, depth_rank.T, target,
            w_in[0], w_hid[0], b_hid[0], w_out[0],
            mom_in[:, 0], mom_hid[:, 0], mom_bias[:, 0], mom_out[:, 0],
        )
    ])
    outs = pl.pallas_call(
        functools.partial(step_kernel, (nbatch, rows_in, rows_hid)),
        out_shape=(
            shape(full_in, hid), shape(2, hid, hid), shape(2, hid), shape(4, hid),
            shape(2, rows_in, hid), shape(2, 2, rows_hid, hid),
            shape(2, 2, rows_hid), shape(2, 4, rows_hid),
        ),
        in_specs=[vmem] * 4,
        out_specs=(vmem,) * 8,
        compiler_params=pltpu.CompilerParams(vmem_limit_bytes=16 * 1024 * 1024),
        name="step",
    )(*sums)
    return tuple(x[None] for x in outs[:4]) + tuple(x[:, None] for x in outs[4:])


def solution(mesh):
    return jax.shard_map(
        body,
        mesh=mesh,
        in_specs=(
            P("region", None, "batch"),
            P("region", "batch"),
            P("region", "batch"),
            P("batch", None),
            P(None, "batch"),
            P("region", "batch", None),
            P("region", None, "batch", None),
            P("region", None, "batch"),
            P("region", None, "batch"),
            P(None, "region", "batch", None),
            P(None, "region", None, "batch", None),
            P(None, "region", None, "batch"),
            P(None, "region", None, "batch"),
        ),
        out_specs=(
            P("region", None, None),
            P("region", None, None, None),
            P("region", None, None),
            P("region", None, None),
            P(None, "region", "batch", None),
            P(None, "region", None, "batch", None),
            P(None, "region", None, "batch"),
            P(None, "region", None, "batch"),
        ),
        check_vma=False,
    )
```

```python
import functools

import jax
import jax.numpy as jnp
from jax import lax
from jax.experimental import pallas as pl
from jax.experimental.pallas import tpu as pltpu
from jax.sharding import PartitionSpec as P

MESH = pl.DeviceIdType.MESH
F32 = jnp.float32
BF16 = jnp.bfloat16
LANES = 128
ONES = 16

beta_first = 0.9
beta_second = 0.95
learn_rate = 0.01
norm_eps = 1e-06
adam_eps = 1e-08


def exact_dot(left, right):
    return jnp.dot(left, right, precision=lax.Precision.HIGHEST, preferred_element_type=F32)


def dot_nt(left, right, precision=None):
    return lax.dot_general(
        left, right, (((1,), (1,)), ((), ())), precision=precision, preferred_element_type=F32
    )


def iota(shape, axis):
    return lax.broadcasted_iota(jnp.int32, shape, axis)


def flip(index, bit):
    return index + bit - 2 * bit * ((index // bit) % 2)


def place_of(row, rows_hid, hid):
    return (iota((rows_hid, hid), 1) == iota((rows_hid, hid), 0) + row * rows_hid).astype(F32)


def kernel(
    cfg,
    feat_hbm, gaps_hbm, counts_hbm, ranks_hbm, target_hbm,
    w_in_hbm, w_hid_hbm, b_hid_hbm, w_out_hbm,
    m_in_hbm, m_hid_hbm, m_bias_hbm, m_out_hbm,
    t1, t2, t3, big,
    feat_raw, gaps_ref, counts_ref, ranks_ref, target_ref,
    w_in_ref, w_hid_ref, b_hid_ref, w_out_ref,
    m_in_ref, m_hid_ref, m_bias_ref, m_out_ref,
    feat, act1, act2, act3, back2, heads, gheads, table,
    w1b, w2b, w3b, w1t, w2t, w3t, wot, early,
    g1, g2, g3, acco, r1, r2, s1, s2, y1, y2, d3,
    in_sem, wsend, wrecv, bsend, brecv, tsend, trecv, gsend, grecv, dsend, drecv,
):
    nbatch, nregion, slots, halves, chunk = cfg
    cell = lax.axis_index("region")
    row = lax.axis_index("batch")
    enc, samples = feat_raw.shape
    hid = w2b.shape[0]
    rows_in, rows_hid = w_in_ref.shape[0], w_hid_ref.shape[1]
    block = rows_in + 2 * rows_hid + 8
    part = samples // halves
    grid = part // LANES
    per_row = LANES // slots
    full_in = feat.shape[0]

    barrier = pltpu.get_barrier_semaphore()
    for k in range(1, nbatch):
        pl.semaphore_signal(
            barrier, inc=1, device_id={"batch": lax.rem(row + k, nbatch)}, device_id_type=MESH
        )
    for k in range(1, nregion):
        pl.semaphore_signal(
            barrier, inc=1, device_id={"region": lax.rem(cell + k, nregion)}, device_id_type=MESH
        )

    origins = (
        w_in_hbm, w_out_hbm, b_hid_hbm, w_hid_hbm, feat_hbm, m_out_hbm, m_bias_hbm, m_in_hbm,
        m_hid_hbm, gaps_hbm, counts_hbm, ranks_hbm, target_hbm,
    )
    landings = (
        w_in_ref, w_out_ref, b_hid_ref, w_hid_ref, feat_raw, m_out_ref, m_bias_ref, m_in_ref,
        m_hid_ref, gaps_ref, counts_ref, ranks_ref, target_ref,
    )
    arrivals = [
        pltpu.make_async_copy(src, dst, in_sem.at[i])
        for i, (src, dst) in enumerate(zip(origins, landings))
    ]
    for arrival in arrivals:
        arrival.start()
    act1[hid:hid + ONES, :] = jnp.ones((ONES, samples), BF16)
    act2[hid:hid + ONES, :] = jnp.ones((ONES, samples), BF16)
    gheads[...] = jnp.zeros_like(gheads)
    g1[...] = jnp.zeros_like(g1)
    g2[...] = jnp.zeros_like(g2)
    g3[...] = jnp.zeros_like(g3)
    acco[...] = jnp.zeros_like(acco)
    for arrival in arrivals:
        arrival.wait()

    w1b[pl.ds(row * rows_in, rows_in), :] = w_in_ref[...].astype(BF16)
    w2b[pl.ds(row * rows_hid, rows_hid), :] = w_hid_ref[0].astype(BF16)
    w3b[pl.ds(row * rows_hid, rows_hid), :] = w_hid_ref[1].astype(BF16)
    place = place_of(row, rows_hid, hid)

    def spread(narrow_out, narrow_bias):
        narrow = jnp.concatenate(
            [narrow_out, narrow_bias, jnp.zeros((2, rows_hid), F32)], axis=0
        )
        return exact_dot(narrow, place)

    own_small = spread(w_out_ref[...], b_hid_ref[...])
    early[row] = own_small
    big[row, 0, 0:rows_in] = w_in_ref[...]
    big[row, 0, rows_in:rows_in + rows_hid] = w_hid_ref[0]
    big[row, 0, rows_in + rows_hid:rows_in + 2 * rows_hid] = w_hid_ref[1]
    big[row, 0, rows_in + 2 * rows_hid:block] = own_small
    for kind in range(2):
        big[row, kind + 1, 0:rows_in] = m_in_ref[kind]
        big[row, kind + 1, rows_in:rows_in + rows_hid] = m_hid_ref[kind, 0]
        big[row, kind + 1, rows_in + rows_hid:rows_in + 2 * rows_hid] = m_hid_ref[kind, 1]
        big[row, kind + 1, rows_in + 2 * rows_hid:block] = spread(m_out_ref[kind], m_bias_ref[kind])

    @pl.loop(0, samples // chunk)
    def _(step):
        span = pl.ds(pl.multiple_of(step * chunk, chunk), chunk)
        wide = feat_raw[:, span].astype(F32)
        feat[:, span] = jnp.concatenate([wide, jnp.ones((1, chunk), F32)], axis=0).astype(BF16)

    pl.semaphore_wait(barrier, nbatch - 1 + nregion - 1)

    pieces = (
        lambda d: w1b.at[pl.ds(d * rows_in, rows_in), :],
        lambda d: early.at[d],
        lambda d: w2b.at[pl.ds(d * rows_hid, rows_hid), :],
        lambda d: w3b.at[pl.ds(d * rows_hid, rows_hid), :],
    )

    def weight_copy(piece, k, origin, target):
        ref = pieces[piece](origin)
        return pltpu.make_async_remote_copy(
            src_ref=ref, dst_ref=ref, send_sem=wsend.at[piece, k], recv_sem=wrecv.at[piece, k],
            device_id={"batch": target}, device_id_type=MESH,
        )

    for piece in (0, 2, 1, 3):
        for k in range(1, nbatch):
            weight_copy(piece, k, row, lax.rem(row + k, nbatch)).start()

    def await_weights(piece):
        for k in range(1, nbatch):
            weight_copy(piece, k, lax.rem(row + nbatch - k, nbatch), row).wait_recv()

    bits = []
    while (1 << len(bits)) < nbatch:
        bits.append(1 << len(bits))
    high = bits[::-1]
    blocks = {}
    count = 0
    known = [0]
    for bit in high:
        blocks[bit] = []
        for held in known:
            blocks[bit].append((held, count))
            count += 1
        known = known + [held ^ bit for held in known]

    def offset(index, mask):
        for bit in bits:
            if mask & bit:
                index = flip(index, bit)
        return index

    def block_copy(bit, held, sem, incoming):
        ref = big.at[offset(row, held ^ bit if incoming else held)]
        return pltpu.make_async_remote_copy(
            src_ref=ref, dst_ref=ref, send_sem=bsend.at[sem], recv_sem=brecv.at[sem],
            device_id={"batch": flip(row, bit)}, device_id_type=MESH,
        )

    for bit in high:
        for held, sem in blocks[bit]:
            if held == 0:
                block_copy(bit, held, sem, False).start()

    square = (LANES, LANES)
    first_lane, second_lane = iota(square, 0), iota(square, 1)
    same = first_lane // slots == second_lane // slots
    upto = (same & (first_lane <= second_lane)).astype(F32)
    beyond = (same & (first_lane > second_lane)).astype(F32)
    to_ray = (first_lane // slots == second_lane % per_row).astype(F32)
    to_slot = (first_lane % per_row == second_lane // slots).astype(F32)
    ranks = ranks_ref[...].astype(F32)
    await_weights(0)
    w1t[...] = w1b[...].astype(F32).T.astype(BF16)

    def over(half, body):
        @pl.loop(0, part // chunk)
        def _(step):
            body(pl.ds(pl.multiple_of(half * part + step * chunk, chunk), chunk), step)

    def first(span, step):
        pre = jnp.dot(w1t[...], feat[:, span], preferred_element_type=F32)
        act1[0:hid, span] = jnp.maximum(pre, 0.0).astype(BF16)

    for half in range(halves):
        over(half, first)
    await_weights(1)
    small = early[0]
    for d in range(1, nbatch):
        small = small + early[d]
    wide_out = small.astype(BF16)
    tall = small.T
    wot[...] = tall.astype(BF16)
    bias_two, bias_three = tall[:, 4:5], tall[:, 5:6]

    def forward(half):
        def second(span, step):
            pre = jnp.dot(w2t[...], act1[0:hid, span], preferred_element_type=F32) + bias_two
            act2[0:hid, span] = jnp.maximum(pre, 0.0).astype(BF16)

        def third(span, step):
            pre = jnp.dot(w3t[...], act2[0:hid, span], preferred_element_type=F32) + bias_three
            act = jnp.maximum(pre, 0.0).astype(BF16)
            act3[:, span] = act
            out = jnp.dot(wide_out, act, preferred_element_type=F32)
            for t in range(chunk // LANES):
                at = half * grid * 8 + step * (chunk // LANES * 8) + t * 8
                heads[pl.ds(pl.multiple_of(at, 8), 8), :] = out[:, t * LANES:(t + 1) * LANES]

        if half == 0:
            await_weights(2)
            w2t[...] = w2b[...].astype(F32).T.astype(BF16)
        over(half, second)
        if half == 0:
            await_weights(3)
            w3t[...] = w3b[...].astype(F32).T.astype(BF16)
        over(half, third)

    def optical(half):
        raw = [heads[pl.ds(half * grid * 8 + k, grid, stride=8), :] for k in range(4)]
        gaps = gaps_ref[half * grid:(half + 1) * grid, :]
        lane, line = iota((grid, LANES), 1), iota((grid, LANES), 0)
        mine = lane // per_row == line + half * grid
        counted = exact_dot(jnp.where(mine, counts_ref[...].astype(F32), 0.0), to_slot)
        live = ((lane % slots).astype(F32) < counted - 0.5).astype(F32)
        softplus = jnp.maximum(raw[0], 0.0) + jnp.log1p(jnp.exp(-jnp.abs(raw[0])))
        depth = softplus * gaps * live
        shade = [jax.nn.sigmoid(raw[k]) for k in (1, 2, 3)]
        cum_in = exact_dot(depth, upto)
        series = depth * (1.0 - depth * (0.5 - depth * (1.0 / 6.0 - depth * (1.0 / 24.0))))
        opacity = jnp.where(depth < 0.02, series, 1.0 - jnp.exp(-depth))
        weight = jnp.exp(-(cum_in - depth)) * opacity
        stacked = jnp.concatenate([weight * shade[k] for k in range(3)] + [-depth], axis=0)
        gathered = exact_dot(stacked, to_ray)
        lines = [
            jnp.sum(
                jnp.where(mine, gathered[k * grid:(k + 1) * grid], 0.0), axis=0, keepdims=True
            )
            for k in range(4)
        ]
        table[half, cell] = jnp.concatenate(lines, axis=0)
        return mine, gaps, live, raw[0], shade, cum_in, weight

    def table_copy(half, k, origin, target):
        ref = table.at[half, origin]
        return pltpu.make_async_remote_copy(
            src_ref=ref, dst_ref=ref, send_sem=tsend.at[half, k], recv_sem=trecv.at[half, k],
            device_id={"region": target}, device_id_type=MESH,
        )

    def composite(half, kept):
        mine, gaps, live, raw, shade, cum_in, weight = kept
        every = [table[half, :, k, :] for k in range(4)]
        prefix = jnp.zeros((nregion, LANES), F32)
        for j in range(nregion):
            prefix = prefix + jnp.where(ranks[j:j + 1] < ranks, every[3][j:j + 1], 0.0)
        reach = jnp.exp(prefix)
        here = iota((nregion, LANES), 0) == cell
        own_rank = jnp.sum(jnp.where(here, ranks, 0.0), axis=0, keepdims=True)
        own_reach = jnp.sum(jnp.where(here, reach, 0.0), axis=0, keepdims=True)
        later = ranks > own_rank
        grad_log = jnp.zeros((1, LANES), F32)
        per_ray = []
        for k in range(3):
            lit = reach * every[k]
            grad_colour = 2.0 * (jnp.sum(lit, axis=0, keepdims=True) - target_ref[k:k + 1])
            behind = jnp.sum(jnp.where(later, lit, 0.0), axis=0, keepdims=True)
            grad_log = grad_log + grad_colour * behind
            per_ray.append(own_reach * grad_colour)
        stacked = jnp.concatenate(
            [jnp.where(mine, x, 0.0) for x in per_ray + [grad_log]], axis=0
        )
        laid = exact_dot(stacked, to_slot)
        grad_seg = [laid[k * grid:(k + 1) * grid] for k in range(3)]
        emit = grad_seg[0] * shade[0] + grad_seg[1] * shade[1] + grad_seg[2] * shade[2]
        after = exact_dot(emit * weight, beyond)
        grad_depth = emit * jnp.exp(-cum_in) - after - laid[3 * grid:4 * grid]
        base = half * grid * 8
        gheads[pl.ds(base, grid, stride=8), :] = grad_depth * live * gaps * jax.nn.sigmoid(raw)
        for k in range(3):
            gheads[pl.ds(base + k + 1, grid, stride=8), :] = (
                grad_seg[k] * weight * shade[k] * (1.0 - shade[k])
            )

    def backward_three(half):
        def body(span, step):
            tiles = []
            for t in range(chunk // LANES):
                at = half * grid * 8 + step * (chunk // LANES * 8) + t * 8
                tiles.append(gheads[pl.ds(pl.multiple_of(at, 8), 8), :])
            grad_heads = jnp.concatenate(tiles, axis=1).astype(BF16)
            act = act3[:, span]
            acco[...] += dot_nt(grad_heads, act)
            raw = jnp.dot(wot[...], grad_heads, preferred_element_type=F32).astype(BF16)
            back3 = jnp.where(act > 0, raw, jnp.zeros_like(raw))
            g1[...] += dot_nt(act2[:, span], back3)
            raw = jnp.dot(w3b[...], back3, preferred_element_type=F32).astype(BF16)
            back2[:, span] = jnp.where(act2[0:hid, span] > 0, raw, jnp.zeros_like(raw))

        over(half, body)

    def grad_two(half):
        def body(span, step):
            g2[...] += dot_nt(act1[:, span], back2[:, span])

        over(half, body)

    def backward_one(half):
        def body(span, step):
            raw = jnp.dot(w2b[...], back2[:, span], preferred_element_type=F32).astype(BF16)
            back1 = jnp.where(act1[0:hid, span] > 0, raw, jnp.zeros_like(raw))
            g3[...] += dot_nt(feat[:, span], back1)

        over(half, body)

    kept = []
    for half in range(halves):
        forward(half)
        kept.append(optical(half))
        for k in range(1, nregion):
            table_copy(half, k, cell, lax.rem(cell + k, nregion)).start()
    for half in range(halves):
        for k in range(1, nregion):
            table_copy(half, k, lax.rem(cell + nregion - k, nregion), cell).wait_recv()
        composite(half, kept[half])
        backward_three(half)

    side = row % 2
    partner = flip(row, 1)

    def grad_copy(src, dst, sem, target):
        return pltpu.make_async_remote_copy(
            src_ref=src, dst_ref=dst, send_sem=gsend.at[sem], recv_sem=grecv.at[sem],
            device_id={"batch": target}, device_id_type=MESH,
        )

    steps = 2 + len(bits) - 1

    def reduce_start(group, g, r):
        length = r.shape[0]
        away = g.at[pl.ds(pl.multiple_of((1 - side) * length, 8), length), :]
        copy = grad_copy(away, r, group * steps, partner)
        copy.start()
        return copy

    def reduce_across(group, g, r, s, y, copy):
        length = r.shape[0]
        copy.wait_recv()
        near = g[pl.ds(pl.multiple_of(side * length, 8), length), :]
        s[0] = (near + r[...]).astype(BF16)
        return [
            grad_copy(s.at[i], y.at[i], group * steps + 1 + i, flip(row, bit))
            for i, bit in enumerate(bits[1:])
        ]

    def reduce_stages(group, s, y, t, copies):
        length = s.shape[1]
        for i, copy in enumerate(copies):
            if i > 0:
                s[i] = total.astype(BF16)
                copy.start()
            copy.wait_recv()
            total = s[i].astype(F32) + y[i].astype(F32)
        span = pl.ds(pl.multiple_of(side * length, 8), length)
        t[span, :] = total
        last = grad_copy(t.at[span, :], t.at[span, :], group * steps + steps - 1, partner)
        last.start()
        return last

    def reduce_end(group, t):
        length = t.shape[0] // 2
        span = pl.ds(pl.multiple_of((1 - side) * length, 8), length)
        grad_copy(t.at[span, :], t.at[span, :], group * steps + steps - 1, partner).wait_recv()

    middle = halves // 2
    g1[hid + 8:hid + ONES, :] = acco[...]
    first_one = reduce_start(0, g1, r1)
    for half in range(middle):
        grad_two(half)
    cross_one = reduce_across(0, g1, r1, s1, y1, first_one)
    for copy in cross_one[:1]:
        copy.start()
    for half in range(middle, halves):
        grad_two(half)
    first_two = reduce_start(1, g2, r2)
    for bit in high[:-1]:
        for held, sem in blocks[bit]:
            block_copy(bit, held, sem, True).wait_recv()
    for held, sem in blocks[high[-1]]:
        if held != 0:
            block_copy(high[-1], held, sem, False).start()
    backward_one(0)
    cross_two = reduce_across(1, g2, r2, s2, y2, first_two)
    for copy in cross_two[:1]:
        copy.start()
    for half in range(1, halves):
        backward_one(half)

    d3[row] = g3[...].astype(BF16)

    def direct_copy(k, origin, target):
        return pltpu.make_async_remote_copy(
            src_ref=d3.at[origin], dst_ref=d3.at[origin], send_sem=dsend.at[k],
            recv_sem=drecv.at[k], device_id={"batch": target}, device_id_type=MESH,
        )

    for k in range(1, nbatch):
        direct_copy(k, row, lax.rem(row + k, nbatch)).start()
    last_one = reduce_stages(0, s1, y1, t1, cross_one)
    last_two = reduce_stages(1, s2, y2, t2, cross_two)
    for k in range(1, nbatch):
        direct_copy(k, lax.rem(row + nbatch - k, nbatch), row).wait_recv()
    total = d3[0].astype(F32)
    for d in range(1, nbatch):
        total = total + d3[d].astype(F32)
    t3[...] = total
    reduce_end(0, t1)
    for held, sem in blocks[high[-1]]:
        block_copy(high[-1], held, sem, True).wait_recv()
    reduce_end(1, t2)

    for piece in range(4):
        for k in range(1, nbatch):
            weight_copy(piece, k, row, lax.rem(row + k, nbatch)).wait_send()
    for bit in high:
        for held, sem in blocks[bit]:
            block_copy(bit, held, sem, False).wait_send()
    for half in range(halves):
        for k in range(1, nregion):
            table_copy(half, k, cell, lax.rem(cell + k, nregion)).wait_send()
    for k in range(1, nbatch):
        direct_copy(k, row, lax.rem(row + k, nbatch)).wait_send()
    for copy in [first_one, first_two, last_one, last_two] + cross_one + cross_two:
        copy.wait_send()


def step_kernel(
    cfg, t1, t2, t3, big, nw_in, nw_hid, nb_hid, nw_out, nm_in, nm_hid, nm_bias, nm_out
):
    nbatch, rows_in, rows_hid = cfg
    row = lax.axis_index("batch")
    full_in, hid = nw_in.shape
    block = big.shape[2]
    place = place_of(row, rows_hid, hid)
    count_all = full_in * hid + 2 * hid * hid + 6 * hid
    last_rows = jnp.concatenate(
        [t1[hid + 8:hid + 12, :], t2[hid:hid + 1, :], t1[hid:hid + 1, :], jnp.zeros((2, hid), F32)],
        axis=0,
    )

    def squares(x):
        return jnp.sum(x * x, axis=0, keepdims=True)

    columns = (
        squares(t1[0:hid, :]) + squares(t2[0:hid, :]) + squares(t3[...])
        + squares(last_rows)
    )
    total_sq = jnp.sum(columns, axis=1, keepdims=True)
    scale = lax.rsqrt(total_sq / count_all + norm_eps)

    def adam(grad, param, first, second):
        scaled = grad * scale
        first = beta_first * first + (1.0 - beta_first) * scaled
        second = beta_second * second + (1.0 - beta_second) * scaled * scaled
        return param - learn_rate * first / (jnp.sqrt(second) + adam_eps), first, second

    def span_of(d, rows, start=0):
        return pl.ds(pl.multiple_of(start + d * rows, 8), rows)

    def update(d, grad, lo, rows):
        return adam(
            grad, big[d, 0, lo:lo + rows], big[d, 1, lo:lo + rows], big[d, 2, lo:lo + rows]
        )

    lo_two, lo_three, lo_small = rows_in, rows_in + rows_hid, rows_in + 2 * rows_hid
    for d in range(nbatch):
        at_in = slice(d * rows_in, (d + 1) * rows_in)
        at_hid = slice(d * rows_hid, (d + 1) * rows_hid)
        nw_in[at_in, :] = update(d, t3[at_in, :], 0, rows_in)[0]
        nw_hid[0, at_hid, :] = update(d, t2[at_hid, :], lo_two, rows_hid)[0]
        nw_hid[1, at_hid, :] = update(d, t1[at_hid, :], lo_three, rows_hid)[0]
    whole = []
    for kind in range(3):
        value = big[0, kind, lo_small:block]
        for d in range(1, nbatch):
            value = value + big[d, kind, lo_small:block]
        whole.append(value)
    fresh, first, second = adam(last_rows, *whole)
    nw_out[...] = fresh[0:4]
    nb_hid[...] = fresh[4:6]
    for kind, value in enumerate((first, second)):
        narrow = dot_nt(value, place, lax.Precision.HIGHEST)
        nm_out[kind] = narrow[0:4]
        nm_bias[kind] = narrow[4:6]
    _, first, second = update(row, t3[span_of(row, rows_in), :], 0, rows_in)
    nm_in[0], nm_in[1] = first, second
    _, first, second = update(row, t2[span_of(row, rows_hid), :], lo_two, rows_hid)
    nm_hid[0, 0], nm_hid[1, 0] = first, second
    _, first, second = update(row, t1[span_of(row, rows_hid), :], lo_three, rows_hid)
    nm_hid[0, 1], nm_hid[1, 1] = first, second


def body(
    features, spacing, counts, depth_rank, target, w_in, w_hid, b_hid, w_out,
    mom_in, mom_hid, mom_bias, mom_out,
):
    nbatch, nregion = lax.axis_size("batch"), lax.axis_size("region")
    _, enc, samples = features.shape
    rays = counts.shape[1]
    slots = samples // rays
    hid = w_in.shape[2]
    rows_in, rows_hid = w_in.shape[1], w_hid.shape[2]
    full_in = rows_in * nbatch
    halves = 2
    chunk = min(2048, samples // halves)
    block = rows_in + 2 * rows_hid + 8
    levels = nbatch.bit_length() - 1
    len1 = (hid + ONES) // 2
    len2 = len1
    cfg = (nbatch, nregion, slots, halves, chunk)
    vmem = pl.BlockSpec(memory_space=pltpu.VMEM)
    shape = lambda *dims: jax.ShapeDtypeStruct(dims, F32)
    dma = pltpu.SemaphoreType.DMA
    crossing = max(levels - 1, 1)
    sums = pl.pallas_call(
        functools.partial(kernel, cfg),
        out_shape=(
            pltpu.VMEM((2 * len1, hid), F32), pltpu.VMEM((2 * len2, hid), F32),
            pltpu.VMEM((full_in, hid), F32), pltpu.VMEM((nbatch, 3, block, hid), F32),
        ),
        in_specs=[pl.BlockSpec(memory_space=pltpu.HBM)] * 13,
        out_specs=(vmem,) * 4,
        scratch_shapes=[
            pltpu.VMEM((enc, samples), BF16),
            pltpu.VMEM((samples // LANES, LANES), F32),
            pltpu.VMEM(counts.shape, jnp.int32),
            pltpu.VMEM((nregion, rays), jnp.int32),
            pltpu.VMEM(target.shape, F32),
            pltpu.VMEM(w_in.shape[1:], F32),
            pltpu.VMEM(w_hid.shape[1:], F32),
            pltpu.VMEM(b_hid.shape[1:], F32),
            pltpu.VMEM(w_out.shape[1:], F32),
            pltpu.VMEM((2,) + mom_in.shape[2:], F32),
            pltpu.VMEM((2,) + mom_hid.shape[2:], F32),
            pltpu.VMEM((2,) + mom_bias.shape[2:], F32),
            pltpu.VMEM((2,) + mom_out.shape[2:], F32),
            pltpu.VMEM((full_in, samples), BF16),
            pltpu.VMEM((hid + ONES, samples), BF16),
            pltpu.VMEM((hid + ONES, samples), BF16),
            pltpu.VMEM((hid, samples), BF16),
            pltpu.VMEM((hid, samples), BF16),
            pltpu.VMEM((samples // LANES * 8, LANES), F32),
            pltpu.VMEM((samples // LANES * 8, LANES), F32),
            pltpu.VMEM((halves, nregion, 4, LANES), F32),
            pltpu.VMEM((full_in, hid), BF16),
            pltpu.VMEM((hid, hid), BF16),
            pltpu.VMEM((hid, hid), BF16),
            pltpu.VMEM((hid, full_in), BF16),
            pltpu.VMEM((hid, hid), BF16),
            pltpu.VMEM((hid, hid), BF16),
            pltpu.VMEM((hid, 8), BF16),
            pltpu.VMEM((nbatch, 8, hid), F32),
            pltpu.VMEM((2 * len1, hid), F32),
            pltpu.VMEM((2 * len2, hid), F32),
            pltpu.VMEM((full_in, hid), F32),
            pltpu.VMEM((8, hid), F32),
            pltpu.VMEM((len1, hid), F32),
            pltpu.VMEM((len2, hid), F32),
            pltpu.VMEM((crossing, len1, hid), BF16),
            pltpu.VMEM((crossing, len2, hid), BF16),
            pltpu.VMEM((crossing, len1, hid), BF16),
            pltpu.VMEM((crossing, len2, hid), BF16),
            pltpu.VMEM((nbatch, full_in, hid), BF16),
            dma((13,)),
            dma((4, nbatch)),
            dma((4, nbatch)),
            dma((nbatch,)),
            dma((nbatch,)),
            dma((halves, nregion)),
            dma((halves, nregion)),
            dma((2 * (levels + 1),)),
            dma((2 * (levels + 1),)),
            dma((nbatch,)),
            dma((nbatch,)),
        ],
        compiler_params=pltpu.CompilerParams(
            collective_id=0, has_side_effects=True, vmem_limit_bytes=44 * 1024 * 1024
        ),
        name="window",
    )(*[
        pltpu.with_memory_space_constraint(x, pltpu.HBM) for x in (
            features[0], spacing.reshape(samples // LANES, LANES), counts, depth_rank.T, target,
            w_in[0], w_hid[0], b_hid[0], w_out[0],
            mom_in[:, 0], mom_hid[:, 0], mom_bias[:, 0], mom_out[:, 0],
        )
    ])
    outs = pl.pallas_call(
        functools.partial(step_kernel, (nbatch, rows_in, rows_hid)),
        out_shape=(
            shape(full_in, hid), shape(2, hid, hid), shape(2, hid), shape(4, hid),
            shape(2, rows_in, hid), shape(2, 2, rows_hid, hid),
            shape(2, 2, rows_hid), shape(2, 4, rows_hid),
        ),
        in_specs=[vmem] * 4,
        out_specs=(vmem,) * 8,
        compiler_params=pltpu.CompilerParams(vmem_limit_bytes=16 * 1024 * 1024),
        name="step",
    )(*sums)
    return tuple(x[None] for x in outs[:4]) + tuple(x[:, None] for x in outs[4:])


def solution(mesh):
    return jax.shard_map(
        body,
        mesh=mesh,
        in_specs=(
            P("region", None, "batch"),
            P("region", "batch"),
            P("region", "batch"),
            P("batch", None),
            P(None, "batch"),
            P("region", "batch", None),
            P("region", None, "batch", None),
            P("region", None, "batch"),
            P("region", None, "batch"),
            P(None, "region", "batch", None),
            P(None, "region", None, "batch", None),
            P(None, "region", None, "batch"),
            P(None, "region", None, "batch"),
        ),
        out_specs=(
            P("region", None, None),
            P("region", None, None, None),
            P("region", None, None),
            P("region", None, None),
            P(None, "region", "batch", None),
            P(None, "region", None, "batch", None),
            P(None, "region", None, "batch"),
            P(None, "region", None, "batch"),
        ),
        check_vma=False,
    )
```
